32 devices in a mesh: groups: 2 (over y), gx: 4 (over z), gy: 2 (over x), gz: 2 (over core).
Axes of the slice: x: 2, y: 2, z: 4, core: 2. Of those that a mesh axis runs over, the one named last changes fastest.
Arguments:
- charge: float32 [128, 64, 256], P(('groups', 'gx'), 'gy', 'gz'), parts along dimension 0, may hold values from -6 to 6
Outputs:
- potential: float32 [128, 64, 256], P(('groups', 'gx'), 'gy', 'gz'), parts along dimension 0
The draws below stay inside these ranges and needn't reach their ends.
There are 2 independent parts, one for each index of `groups`. The reference program is written for one: setup_inputs(seed, part) draws one part's arguments, and reference() takes and returns one part's arrays. A program takes and returns all parts, laid end to end along the dimension named above; each array names one. Nothing has to cross between parts.
All inputs are finite; a program needn't handle non-finite values.
Results may differ from the reference program's by a relative error of at most 0.0001.
Values sent between devices are 32-bit elements; how exact they have to be, the bound alone decides.
A program may use at most 128 MiB of HBM per device.

```python
import jax
import jax.numpy as jnp

CYCLES = 2
SWEEPS = 2
SLEV = 4
RLEV = 3
NX = 64
NY = 64
NZ = 256


def block_levels(own_key, extent, pieces, low, top_value):
    level = 1.0
    for dim, parts in pieces:
        heights = jax.random.uniform(jax.random.fold_in(jax.random.fold_in(own_key, 6), dim), (parts,), jnp.float32, low / len(pieces), top_value / len(pieces))
        level = level * jnp.repeat(jnp.exp(heights), extent[dim] // parts).reshape((-1,) + (1,) * (len(extent) - 1 - dim))
    return level


def gaussian(key, shape, scale, most, pieces=(), dtype=jnp.bfloat16):
    drawn = jax.random.normal(key, shape, jnp.float32) * scale
    if len(pieces) > 0:
        drawn = block_levels(key, shape, pieces, -0.22, 0.18) * drawn
    return jnp.clip(drawn, min=-most, max=most).astype(dtype)


def setup_inputs(seed: int = 0, part: int = 0) -> dict:
    streams_of = jax.random.split(jax.random.key(seed), 2)
    part_splits = jax.random.split(jax.random.fold_in(streams_of[1], part), 2)
    return {
        "charge": gaussian(part_splits[0], (NX, NY, NZ), 1.0, 6.0, ((0, 4), (1, 2), (2, 2)), jnp.float32),
    }


OMEGA = 2.0 / 3.0
SCREEN = 0.001


def operate(field, scale):
    beside_all = jnp.roll(field, 1, 0) + jnp.roll(field, -1, 0)
    beside_all = beside_all + jnp.roll(field, 1, 1) + jnp.roll(field, -1, 1)
    beside_all = beside_all + jnp.roll(field, 1, 2) + jnp.roll(field, -1, 2)
    return (6.0 * field - beside_all) * scale + SCREEN * field


def relax(field, source, scale):
    return field + OMEGA * (source - operate(field, scale)) / (6.0 * scale + SCREEN)


def restrict(field):
    size_x, size_y, size_z = field.shape
    blocks = field.reshape(size_x // 2, 2, size_y // 2, 2, size_z // 2, 2)
    return blocks.mean(axis=(1, 3, 5))


def prolong(field):
    return jnp.repeat(jnp.repeat(jnp.repeat(field, 2, 0), 2, 1), 2, 2)


def cycle(level, source, field):
    scale = 0.25 ** level
    for sweep in range(SWEEPS):
        field = relax(field, source, scale)
    if level == SLEV + RLEV - 1:
        return field
    residual = source - operate(field, scale)
    coarse_rhs = restrict(residual)
    correction = cycle(level + 1, coarse_rhs, jnp.zeros(coarse_rhs.shape, jnp.float32))
    field = field + prolong(correction)
    for sweep in range(SWEEPS):
        field = relax(field, source, scale)
    return field


def reference(charge):
    potential = jnp.zeros(charge.shape, jnp.float32)
    for turn in range(CYCLES):
        potential = cycle(0, charge, potential)
    return potential
```

```python
import functools

import jax
import jax.numpy as jnp
from jax import lax
from jax.experimental import pallas as pl
from jax.experimental.pallas import tpu as pltpu
from jax.sharding import PartitionSpec as P

CYCLES = 2
LEVELS = 7

OMEGA = 2.0 / 3.0
SCREEN = 0.001

HALO = 8
SENT = 7
ROWS = 8
WIDE = 8
LANES = 128
MESH = pl.DeviceIdType.MESH


def factors(level):
    scale = 0.25**level
    diagonal = 6.0 * scale + SCREEN
    return scale, diagonal, OMEGA / diagonal, OMEGA * scale / diagonal


def roll(value, shift, axis):
    size = value.shape[axis]
    return value if size == 1 else pltpu.roll(value, shift % size, axis)


def split_dot(value, matrix):
    high = value.astype(jnp.bfloat16)
    low = (value - high.astype(jnp.float32)).astype(jnp.bfloat16)
    dot = functools.partial(jnp.dot, preferred_element_type=jnp.float32)
    return dot(high, matrix) + dot(low, matrix)


def dot_lanes(value, matrix):
    shape = value.shape
    out = split_dot(value.reshape(-1, shape[-1]), matrix)
    return out.reshape(shape[:-1] + (matrix.shape[-1],))


def indicator(rows, columns, rule):
    i = lax.broadcasted_iota(jnp.int32, (rows, columns), 0)
    j = lax.broadcasted_iota(jnp.int32, (rows, columns), 1)
    return jnp.where(rule(i, j), 1.0, 0.0).astype(jnp.bfloat16)


def plane_sum(value):
    last = value.ndim - 1
    total = roll(value, 1, last - 1) + roll(value, -1, last - 1)
    return total + (roll(value, 1, last) + roll(value, -1, last))


def inner_sum(value):
    return value[:-2] + value[2:] + plane_sum(value[1:-1])


def wrap_sum(value):
    if value.shape[0] == 1:
        beside = value + value
    else:
        beside = jnp.concatenate([value[-1:], value[:-1]], 0) + jnp.concatenate([value[1:], value[:1]], 0)
    return beside + plane_sum(value)


def kernel(sizes, charge_ref, out_ref, raw, src, va, vb, pairs, tall, f1_local, f1, v1, w1, sum1, slots,
           chunks, window, mats, split_mat, join_mat, staged, *rest):
    n_gx, n_gy, n_gz = sizes
    n_levels = LEVELS - 2
    fs, vs, ts, us = (rest[k * n_levels:(k + 1) * n_levels] for k in range(4))
    (send0, recv0, send1, recv1, send2, recv2, send3, recv3) = rest[4 * n_levels:]
    ix, iy, iz = lax.axis_index("gx"), lax.axis_index("gy"), lax.axis_index("gz")
    bx, cy, cz = charge_ref.shape
    by = cy // n_gz
    n_yb = n_gy * n_gz
    x0, r0 = bx + 2 * HALO, by + 2 * ROWS
    b1x, b1y = bx // 2, by // 2
    b2x, b2y = b1x // 2, b1y // 2
    nx2 = b2x * n_gx
    iyb = iy * n_gz + iz
    other = 1 - iz

    def place(x, yb):
        x = lax.rem(x + n_gx, n_gx)
        yb = lax.rem(yb + n_yb, n_yb)
        return {"gx": x, "gy": lax.div(yb, n_gz), "gz": lax.rem(yb, n_gz)}

    peers = [(dx, dyb) for dx in range(n_gx) for dyb in range(n_yb) if (dx, dyb) != (0, 0)]
    barrier = pltpu.get_barrier_semaphore()
    for dx, dyb in peers:
        pl.semaphore_signal(barrier, inc=1, device_id=place(ix + dx, iyb + dyb), device_id_type=MESH)
    pl.semaphore_wait(barrier, len(peers))

    first = []
    waits = []
    for k, dx in enumerate((-1, 0, 1)):
        planes = bx if dx == 0 else SENT
        from_x = 0 if dx < 1 else bx - SENT
        to_x = {-1: HALO + bx, 0: HALO, 1: HALO - SENT}[dx]
        for t, zt in enumerate((other, iz)):
            from_y = pl.multiple_of((by - ROWS) * zt, 8)
            to_y = pl.multiple_of(ROWS * (1 - zt), 8)
            source = charge_ref.at[pl.ds(from_x, planes), pl.ds(from_y, by + ROWS), :]
            target = raw.at[iz, pl.ds(to_x, planes), pl.ds(to_y, by + ROWS), :]
            if dx == 0 and t == 1:
                pltpu.make_async_copy(source, target, recv0.at[k, 0, iz]).start()
            else:
                first.append(pltpu.make_async_remote_copy(
                    src_ref=source, dst_ref=target, send_sem=send0.at[k, t], recv_sem=recv0.at[k, 0, iz],
                    device_id=place(ix + dx, iy * n_gz + zt), device_id_type=MESH))
        for t, (step, from_y, to_y) in enumerate(((-1, 0, r0 - ROWS), (n_gz, cy - ROWS, 0))):
            first.append(pltpu.make_async_remote_copy(
                src_ref=charge_ref.at[pl.ds(from_x, planes), pl.ds(from_y, ROWS), :],
                dst_ref=raw.at[iz, pl.ds(to_x, planes), pl.ds(to_y, ROWS), :],
                send_sem=send0.at[k, 2 + t], recv_sem=recv0.at[k, 1, iz],
                device_id=place(ix + dx, iy * n_gz + step), device_id_type=MESH))
        for z in range(n_gz):
            own = raw.at[z, pl.ds(to_x, planes), pl.ds(pl.multiple_of(ROWS * other, 8), by + ROWS), :]
            side = raw.at[z, pl.ds(to_x, planes), pl.ds(pl.multiple_of((r0 - ROWS) * iz, 8), ROWS), :]
            waits.append(pltpu.make_async_copy(own, own, recv0.at[k, 0, z]))
            waits.append(pltpu.make_async_copy(side, side, recv0.at[k, 1, z]))
    for copy in first:
        copy.start()

    nz = n_gz * cz
    half = nz // 2
    split_mat[...] = indicator(nz, nz, lambda i, j: i == jnp.where(j < half, 2 * j, 2 * (j - half) + 1))
    join_mat[...] = indicator(nz, nz, lambda i, j: j == jnp.where(i < half, 2 * i, 2 * (i - half) + 1))
    for level in range(1, LEVELS - 1):
        period = nz >> level
        mats[level - 1, 0] = indicator(
            LANES, LANES, lambda i, j: lax.div(i, 2) == (j & (period // 2 - 1)) + jnp.where(i < period, 0, LANES))
        mats[level - 1, 1] = indicator(LANES, LANES, lambda i, j: i == lax.div(j & (period - 1), 2))

    for wait in waits:
        wait.wait()

    filled = bx + 2 * SENT
    step = max(d for d in range(1, 7) if filled % d == 0)

    def deal(c, _):
        planes = pl.ds(HALO - SENT + step * c, step)
        value = jnp.concatenate([raw[0, planes], raw[1, planes]], -1)
        value = dot_lanes(value, split_mat[...])
        src[0, planes] = value[..., :half]
        src[1, planes] = value[..., half:]
        return _

    lax.fori_loop(0, filled // step, deal, None)

    def neighbours(ref, p):
        even, odd = ref[0, p], ref[1, p]
        rows = lambda value: roll(value, 1, 0) + roll(value, -1, 0)
        sum_even = (ref[0, p - 1] + ref[0, p + 1]) + rows(even) + (odd + roll(odd, 1, 1))
        sum_odd = (ref[1, p - 1] + ref[1, p + 1]) + rows(odd) + (even + roll(even, -1, 1))
        return (even, odd), (sum_even, sum_odd)

    def over(extent, body):
        low = HALO - extent

        def pair(c, _):
            p = low + 2 * c
            body(p, c)
            return _

        lax.fori_loop(0, (bx + 2 * extent) // 2, pair, None)

    scale0, diag0, alpha0, beta0 = factors(0)

    def begin0(ref, extent):
        def body(p, c):
            for q in (p, p + 1):
                centre, beside = neighbours(src, q)
                for z in range(2):
                    ref[z, q] = alpha0 * ((2.0 - OMEGA) * centre[z] + beta0 * beside[z])

        over(extent, body)

    def sweep0(old, new, extent):
        def body(p, c):
            for q in (p, p + 1):
                centre, beside = neighbours(old, q)
                for z in range(2):
                    new[z, q] = (1.0 - OMEGA) * centre[z] + alpha0 * src[z, q] + beta0 * beside[z]

        over(extent, body)

    def residual0(ref, extent):
        def body(p, c):
            total = None
            for q in (p, p + 1):
                centre, beside = neighbours(ref, q)
                for z in range(2):
                    term = src[z, q] - diag0 * centre[z] + scale0 * beside[z]
                    total = term if total is None else total + term
            pairs[c] = total

        over(extent, body)
        count = (bx + 2 * extent) // 2
        return 0.125 * (pairs[pl.ds(0, count), pl.ds(0, r0 // 2, stride=2), :]
                        + pairs[pl.ds(0, count), pl.ds(1, r0 // 2, stride=2), :])

    def correct0(ref, extent):
        low1 = WIDE - extent // 2 - extent % 2
        count = b1x + 2 * (WIDE - low1)
        row1 = WIDE - ROWS // 2
        value = v1[pl.ds(low1, count), pl.ds(row1, r0 // 2), :]
        tall[pl.ds(0, count), pl.ds(0, r0 // 2, stride=2), :] = value
        tall[pl.ds(0, count), pl.ds(1, r0 // 2, stride=2), :] = value
        start = HALO - 2 * (WIDE - low1)

        def body(c, _):
            term = tall[c]
            for q in range(2):
                for z in range(2):
                    ref[z, start + 2 * c + q] = ref[z, start + 2 * c + q] + term
            return _

        lax.fori_loop(0, count, body, None)

    scale1, diag1, alpha1, beta1 = factors(1)

    def span(extent):
        return slice(WIDE - extent, WIDE + b1x + extent)

    def begin1(source, extent):
        f = source[span(extent + 1)]
        return alpha1 * ((2.0 - OMEGA) * f[1:-1] + beta1 * inner_sum(f))

    def sweep1(old, source, extent):
        v = old[span(extent + 1)]
        return (1.0 - OMEGA) * v[1:-1] + alpha1 * source[span(extent)] + beta1 * inner_sum(v)

    def residual1(source):
        v = v1[span(1)]
        r = source[span(0)] - diag1 * v[1:-1] + scale1 * inner_sum(v)
        r = r.reshape((b2x, 2) + r.shape[1:]).sum(1)
        sum1[...] = r
        r = (sum1[:, pl.ds(WIDE, b2y, stride=2), :] + sum1[:, pl.ds(WIDE + 1, b2y, stride=2), :]) * 0.125
        return r

    def coarse(k):
        level = k + 2
        scale, diagonal, alpha, beta = factors(level)
        f = fs[k][...]
        v = alpha * ((2.0 - OMEGA) * f + beta * wrap_sum(f))
        if k == n_levels - 1:
            vs[k][...] = v
            return
        r = f - diagonal * v + scale * wrap_sum(v)
        vs[k][...] = v
        rows = r.shape[1]
        us[k][...] = r.reshape((r.shape[0] // 2, 2) + r.shape[1:]).sum(1)
        r = us[k][:, pl.ds(0, rows // 2, stride=2), :] + us[k][:, pl.ds(1, rows // 2, stride=2), :]
        if rows == 8:
            r = jnp.concatenate([r, r], 1)
        fs[k + 1][...] = 0.125 * dot_lanes(r, mats[level - 1, 0])
        coarse(k + 1)
        c = dot_lanes(vs[k + 1][...], mats[level - 1, 1])[:, : rows // 2]
        ts[k][:, pl.ds(0, rows // 2, stride=2), :] = c
        ts[k][:, pl.ds(1, rows // 2, stride=2), :] = c
        c = ts[k][...]
        c = jnp.broadcast_to(c[:, None], (c.shape[0], 2) + c.shape[1:]).reshape(v.shape)
        v = vs[k][...] + c
        for sweep in range(2):
            v = (1.0 - OMEGA) * v + alpha * fs[k][...] + beta * wrap_sum(v)
        vs[k][...] = v

    lane = lax.broadcasted_iota(jnp.int32, (8, LANES), 1)
    me = ix * n_yb + iyb
    begin0(va, SENT - 1)
    done = []
    for cycle in range(CYCLES):
        last = cycle == CYCLES - 1
        ahead = 4 if cycle == 0 else 0
        reach = 4 if last else 6
        rhs = residual0(va, ahead)
        low = WIDE - ahead // 2
        row1 = WIDE - ROWS // 2
        f1_here = f1.at[cycle]
        f1_here[pl.ds(WIDE, b1x), pl.ds(WIDE, b1y), :] = rhs[ahead // 2: ahead // 2 + b1x, WIDE - row1: WIDE - row1 + b1y]
        exchange = []
        for k, (dx, dy) in enumerate([(a, b) for a in (-1, 0, 1) for b in (-1, 0, 1) if (a, b) != (0, 0)]):
            planes = b1x if dx == 0 else reach
            from_x = WIDE + (b1x - reach if dx == 1 else 0)
            to_x = {-1: WIDE + b1x, 0: WIDE, 1: WIDE - reach}[dx]
            exchange.append(pltpu.make_async_remote_copy(
                src_ref=f1_here.at[pl.ds(from_x, planes), pl.ds(WIDE, b1y), :],
                dst_ref=f1_here.at[pl.ds(to_x, planes), pl.ds(WIDE - dy * b1y, b1y), :],
                send_sem=send1.at[cycle, k], recv_sem=recv1.at[cycle, k],
                device_id=place(ix + dx, iyb + dy), device_id_type=MESH))
        if cycle == 0:
            f1_local[pl.ds(low, rhs.shape[0]), pl.ds(row1, r0 // 2), :] = rhs
            down = f1_local
        else:
            for copy in exchange:
                copy.start()
            for copy in exchange:
                copy.wait_recv()
            down = f1_here
        v1[span(1)] = begin1(down, 1)
        rhs2 = dot_lanes(residual1(down).reshape(b2x * b2y, LANES), mats[0, 0])
        count = b2x * b2y // 2
        slots[cycle, me] = jnp.where(lane < LANES // 2, rhs2[:count], rhs2[count:])
        gather = []
        for k, (dx, dyb) in enumerate(peers):
            gather.append(pltpu.make_async_remote_copy(
                src_ref=slots.at[cycle, me], dst_ref=slots.at[cycle, me],
                send_sem=send2.at[cycle, k], recv_sem=recv2.at[cycle, me],
                device_id=place(ix + dx, iyb + dyb), device_id_type=MESH))
        for copy in gather:
            copy.start()
        if cycle == 0:
            for copy in exchange:
                copy.start()
        for dx, dyb in peers:
            who = lax.rem(ix + dx, n_gx) * n_yb + lax.rem(iyb + dyb, n_yb)
            slot = slots.at[cycle, who]
            pltpu.make_async_copy(slot, slot, recv2.at[cycle, who]).wait()
        for x in range(n_gx):
            for yb in range(n_yb):
                tile = slots[cycle, x * n_yb + yb]
                turned = roll(tile, LANES // 2, 1)
                parts = (jnp.where(lane < LANES // 2, tile, turned), jnp.where(lane < LANES // 2, turned, tile))
                for a in range(b2x):
                    part = parts[a // (b2x // 2)]
                    row = (a % (b2x // 2)) * b2y
                    fs[0][x * b2x + a, pl.ds(yb * b2y, b2y), :] = part[row: row + b2y]
        coarse(0)
        solved = dot_lanes(vs[0][...], mats[0, 1])
        for yb in range(n_yb):
            chunks[yb, :, pl.ds(0, b2y), :] = solved[:, yb * b2y:(yb + 1) * b2y]
        for a in range(2 * (WIDE // 2) + b2x):
            xa = lax.rem(ix * b2x - WIDE // 2 + a + nx2, nx2)
            for j in range(3):
                part = chunks[lax.rem(iyb + j - 1 + n_yb, n_yb), xa, pl.ds(0, b2y), :]
                window[a, pl.ds(j * b1y, b2y, stride=2), :] = part
                window[a, pl.ds(j * b1y + 1, b2y, stride=2), :] = part
        if cycle == 0:
            for copy in exchange:
                copy.wait_recv()
        top = reach - 1
        v = begin1(f1_here, top)
        first_plane, planes = WIDE - top, b1x + 2 * top
        wide = window[first_plane // 2: (first_plane + planes + 1) // 2]
        wide = jnp.broadcast_to(wide[:, None], (wide.shape[0], 2) + wide.shape[1:]).reshape((-1,) + wide.shape[1:])
        v1[span(top)] = v + wide[first_plane % 2: first_plane % 2 + planes]
        w1[span(top - 1)] = sweep1(v1, f1_here, top - 1)
        v1[span(top - 2)] = sweep1(w1, f1_here, top - 2)
        done += exchange + gather
        if last:
            correct0(va, 2)
            sweep0(va, vb, 1)
            sweep0(vb, va, 0)
        else:
            correct0(va, SENT - 1)
            sweep0(va, vb, SENT - 2)
            sweep0(vb, va, SENT - 3)
            sweep0(va, vb, SENT - 4)
            sweep0(vb, va, SENT - 5)

    def join(c, _):
        p = HALO + 4 * c
        value = jnp.concatenate([va[z, pl.ds(p, 4), pl.ds(ROWS, by), :] for z in range(2)], -1)
        value = dot_lanes(value, join_mat[...])
        staged[0, pl.ds(4 * c, 4)] = value[..., :half]
        staged[1, pl.ds(4 * c, 4)] = value[..., half:]
        return _

    lax.fori_loop(0, bx // 4, join, None)
    mine = pl.ds(pl.multiple_of(by * iz, 8), by)
    sent = pltpu.make_async_remote_copy(
        src_ref=staged.at[other], dst_ref=out_ref.at[:, mine, :], send_sem=send3.at[0], recv_sem=recv3.at[0],
        device_id=place(ix, iy * n_gz + other), device_id_type=MESH)
    sent.start()
    kept = pltpu.make_async_copy(staged.at[iz], out_ref.at[:, mine, :], recv3.at[1])
    kept.start()
    for copy in first + done:
        copy.wait_send()
    kept.wait()
    sent.wait()


def local(sizes, charge):
    n_gx, n_gy, n_gz = sizes
    bx, cy, cz = charge.shape
    by = cy // n_gz
    n_yb = n_gy * n_gz
    assert n_gz == 2 and cz == LANES and by % 16 == 0 and by // 4 * (bx // 4) == 16
    f32 = jnp.float32
    x0, r0 = bx + 2 * HALO, by + 2 * ROWS
    x1, r1 = bx // 2 + 2 * WIDE, by // 2 + 2 * WIDE
    nx2, ny2 = bx // 4 * n_gx, by // 4 * n_yb
    n_dev = n_gx * n_yb
    n_levels = LEVELS - 2
    shapes = [(nx2 >> k, max(8, ny2 >> k), LANES) for k in range(n_levels)]
    vmem = lambda *shape: pltpu.VMEM(shape, f32)
    level0 = vmem(2, x0, r0, LANES)
    nz = n_gz * cz
    scratch = [
        level0, level0, level0, level0,
        vmem(x0 // 2, r0, LANES), vmem(x0 // 2, r0, LANES),
        vmem(x1, r1, LANES), vmem(CYCLES, x1, r1, LANES), vmem(x1, r1, LANES), vmem(x1, r1, LANES),
        vmem(bx // 4, r1, LANES),
        vmem(CYCLES, n_dev, 8, LANES),
        vmem(n_yb, nx2, 8, LANES),
        vmem(bx // 4 + WIDE, r1, LANES),
        pltpu.VMEM((LEVELS - 2, 2, LANES, LANES), jnp.bfloat16),
        pltpu.VMEM((nz, nz), jnp.bfloat16), pltpu.VMEM((nz, nz), jnp.bfloat16),
        vmem(2, bx, by, LANES),
    ]
    scratch += [vmem(*s) for s in shapes] * 2
    halves = [vmem(max(1, s[0] // 2), s[1], s[2]) for s in shapes]
    scratch += halves * 2
    dma = lambda *shape: pltpu.SemaphoreType.DMA(shape)
    scratch += [dma(3, 4), dma(3, 2, 2), dma(CYCLES, 8), dma(CYCLES, 8),
                dma(CYCLES, n_dev), dma(CYCLES, n_dev), dma(1), dma(2)]
    return pl.pallas_call(
        functools.partial(kernel, sizes),
        out_shape=jax.ShapeDtypeStruct(charge.shape, f32),
        in_specs=[pl.BlockSpec(memory_space=pl.ANY)],
        out_specs=pl.BlockSpec(memory_space=pl.ANY),
        scratch_shapes=scratch,
        compiler_params=pltpu.CompilerParams(collective_id=0, has_side_effects=True),
    )(charge)


def solution(mesh):
    sizes = (mesh.shape["gx"], mesh.shape["gy"], mesh.shape["gz"])
    return jax.shard_map(
        functools.partial(local, sizes),
        mesh=mesh,
        in_specs=(P(("groups", "gx"), "gy", "gz"),),
        out_specs=P(("groups", "gx"), "gy", "gz"),
        check_vma=False,
    )
```

```python
import functools

import jax
import jax.numpy as jnp
from jax import lax
from jax.experimental import pallas as pl
from jax.experimental.pallas import tpu as pltpu
from jax.sharding import PartitionSpec as P

CYCLES = 2
LEVELS = 7

OMEGA = 2.0 / 3.0
SCREEN = 0.001

HALO = 8
SENT = 7
ROWS = 8
WIDE = 8
LANES = 128
MESH = pl.DeviceIdType.MESH


def factors(level):
    scale = 0.25**level
    diagonal = 6.0 * scale + SCREEN
    return scale, diagonal, OMEGA / diagonal, OMEGA * scale / diagonal


def roll(value, shift, axis):
    size = value.shape[axis]
    return value if size == 1 else pltpu.roll(value, shift % size, axis)


def split_dot(value, matrix):
    high = value.astype(jnp.bfloat16)
    low = (value - high.astype(jnp.float32)).astype(jnp.bfloat16)
    dot = functools.partial(jnp.dot, preferred_element_type=jnp.float32)
    return dot(high, matrix) + dot(low, matrix)


def dot_lanes(value, matrix):
    shape = value.shape
    out = split_dot(value.reshape(-1, shape[-1]), matrix)
    return out.reshape(shape[:-1] + (matrix.shape[-1],))


def indicator(rows, columns, rule):
    i = lax.broadcasted_iota(jnp.int32, (rows, columns), 0)
    j = lax.broadcasted_iota(jnp.int32, (rows, columns), 1)
    return jnp.where(rule(i, j), 1.0, 0.0).astype(jnp.bfloat16)


def plane_sum(value):
    last = value.ndim - 1
    total = roll(value, 1, last - 1) + roll(value, -1, last - 1)
    return total + (roll(value, 1, last) + roll(value, -1, last))


def inner_sum(value):
    return value[:-2] + value[2:] + plane_sum(value[1:-1])


def wrap_sum(value):
    if value.shape[0] == 1:
        beside = value + value
    else:
        beside = jnp.concatenate([value[-1:], value[:-1]], 0) + jnp.concatenate([value[1:], value[:1]], 0)
    return beside + plane_sum(value)


def kernel(sizes, charge_ref, out_ref, raw, src, va, vb, pairs, tall, f1_local, f1, v1, w1, sum1, slots,
           chunks, window, mats, split_mat, join_mat, staged, *rest):
    n_gx, n_gy, n_gz = sizes
    n_levels = LEVELS - 2
    fs, vs, ts, us = (rest[k * n_levels:(k + 1) * n_levels] for k in range(4))
    (send0, recv0, send1, recv1, send2, recv2, send3, recv3) = rest[4 * n_levels:]
    ix, iy, iz = lax.axis_index("gx"), lax.axis_index("gy"), lax.axis_index("gz")
    bx, cy, cz = charge_ref.shape
    by = cy // n_gz
    n_yb = n_gy * n_gz
    x0, r0 = bx + 2 * HALO, by + 2 * ROWS
    b1x, b1y = bx // 2, by // 2
    b2x, b2y = b1x // 2, b1y // 2
    nx2 = b2x * n_gx
    iyb = iy * n_gz + iz
    other = 1 - iz

    def place(x, yb):
        x = lax.rem(x + n_gx, n_gx)
        yb = lax.rem(yb + n_yb, n_yb)
        return {"gx": x, "gy": lax.div(yb, n_gz), "gz": lax.rem(yb, n_gz)}

    peers = [(dx, dyb) for dx in range(n_gx) for dyb in range(n_yb) if (dx, dyb) != (0, 0)]
    barrier = pltpu.get_barrier_semaphore()
    for dx, dyb in peers:
        pl.semaphore_signal(barrier, inc=1, device_id=place(ix + dx, iyb + dyb), device_id_type=MESH)
    pl.semaphore_wait(barrier, len(peers))

    first = []
    waits = [[], [], []]
    for k, dx in ((1, 0), (0, -1), (2, 1)):
        planes = bx if dx == 0 else SENT
        from_x = 0 if dx < 1 else bx - SENT
        to_x = {-1: HALO + bx, 0: HALO, 1: HALO - SENT}[dx]
        for t, zt in enumerate((other, iz)):
            from_y = pl.multiple_of((by - ROWS) * zt, 8)
            to_y = pl.multiple_of(ROWS * (1 - zt), 8)
            source = charge_ref.at[pl.ds(from_x, planes), pl.ds(from_y, by + ROWS), :]
            target = raw.at[iz, pl.ds(to_x, planes), pl.ds(to_y, by + ROWS), :]
            if dx == 0 and t == 1:
                pltpu.make_async_copy(source, target, recv0.at[k, 0, iz]).start()
            else:
                first.append(pltpu.make_async_remote_copy(
                    src_ref=source, dst_ref=target, send_sem=send0.at[k, t], recv_sem=recv0.at[k, 0, iz],
                    device_id=place(ix + dx, iy * n_gz + zt), device_id_type=MESH))
        for t, (step, from_y, to_y) in enumerate(((-1, 0, r0 - ROWS), (n_gz, cy - ROWS, 0))):
            first.append(pltpu.make_async_remote_copy(
                src_ref=charge_ref.at[pl.ds(from_x, planes), pl.ds(from_y, ROWS), :],
                dst_ref=raw.at[iz, pl.ds(to_x, planes), pl.ds(to_y, ROWS), :],
                send_sem=send0.at[k, 2 + t], recv_sem=recv0.at[k, 1, iz],
                device_id=place(ix + dx, iy * n_gz + step), device_id_type=MESH))
        for z in range(n_gz):
            own = raw.at[z, pl.ds(to_x, planes), pl.ds(pl.multiple_of(ROWS * other, 8), by + ROWS), :]
            side = raw.at[z, pl.ds(to_x, planes), pl.ds(pl.multiple_of((r0 - ROWS) * iz, 8), ROWS), :]
            waits[k].append(pltpu.make_async_copy(own, own, recv0.at[k, 0, z]))
            waits[k].append(pltpu.make_async_copy(side, side, recv0.at[k, 1, z]))
    for copy in first:
        copy.start()
    near = waits[1]
    far = waits[0] + waits[2]

    nz = n_gz * cz
    half = nz // 2
    split_mat[...] = indicator(nz, nz, lambda i, j: i == jnp.where(j < half, 2 * j, 2 * (j - half) + 1))
    join_mat[...] = indicator(nz, nz, lambda i, j: j == jnp.where(i < half, 2 * i, 2 * (i - half) + 1))
    for level in range(1, LEVELS - 1):
        period = nz >> level
        mats[level - 1, 0] = indicator(
            LANES, LANES, lambda i, j: lax.div(i, 2) == (j & (period // 2 - 1)) + jnp.where(i < period, 0, LANES))
        mats[level - 1, 1] = indicator(LANES, LANES, lambda i, j: i == lax.div(j & (period - 1), 2))

    def deal(start, count, step):
        def body(c, _):
            planes = pl.ds(start + step * c, step)
            value = jnp.concatenate([raw[0, planes], raw[1, planes]], -1)
            value = dot_lanes(value, split_mat[...])
            src[0, planes] = value[..., :half]
            src[1, planes] = value[..., half:]
            return _

        lax.fori_loop(0, count // step, body, None, unroll=True)

    def neighbours(ref, p):
        even, odd = ref[0, p], ref[1, p]
        rows = lambda value: roll(value, 1, 0) + roll(value, -1, 0)
        sum_even = (ref[0, p - 1] + ref[0, p + 1]) + rows(even) + (odd + roll(odd, 1, 1))
        sum_odd = (ref[1, p - 1] + ref[1, p + 1]) + rows(odd) + (even + roll(even, -1, 1))
        return (even, odd), (sum_even, sum_odd)

    def over(extent, body):
        low = HALO - extent

        def pair(c, _):
            p = low + 2 * c
            body(p, c)
            return _

        lax.fori_loop(0, (bx + 2 * extent) // 2, pair, None, unroll=4)

    scale0, diag0, alpha0, beta0 = factors(0)

    def begin0(ref, start, count):
        def body(c, _):
            centre, beside = neighbours(src, start + c)
            for z in range(2):
                ref[z, start + c] = alpha0 * ((2.0 - OMEGA) * centre[z] + beta0 * beside[z])
            return _

        lax.fori_loop(0, count, body, None, unroll=7)

    def sweep0(old, new, extent):
        def body(p, c):
            for q in (p, p + 1):
                centre, beside = neighbours(old, q)
                for z in range(2):
                    new[z, q] = (1.0 - OMEGA) * centre[z] + alpha0 * src[z, q] + beta0 * beside[z]

        over(extent, body)

    def residual0(ref, extent):
        def body(p, c):
            total = None
            for q in (p, p + 1):
                centre, beside = neighbours(ref, q)
                for z in range(2):
                    term = src[z, q] - diag0 * centre[z] + scale0 * beside[z]
                    total = term if total is None else total + term
            pairs[c] = total

        over(extent, body)
        count = (bx + 2 * extent) // 2
        return 0.125 * (pairs[pl.ds(0, count), pl.ds(0, r0 // 2, stride=2), :]
                        + pairs[pl.ds(0, count), pl.ds(1, r0 // 2, stride=2), :])

    def correct0(ref, extent):
        low1 = WIDE - extent // 2 - extent % 2
        count = b1x + 2 * (WIDE - low1)
        row1 = WIDE - ROWS // 2
        value = v1[pl.ds(low1, count), pl.ds(row1, r0 // 2), :]
        tall[pl.ds(0, count), pl.ds(0, r0 // 2, stride=2), :] = value
        tall[pl.ds(0, count), pl.ds(1, r0 // 2, stride=2), :] = value
        start = HALO - 2 * (WIDE - low1)

        def body(c, _):
            term = tall[c]
            for q in range(2):
                for z in range(2):
                    ref[z, start + 2 * c + q] = ref[z, start + 2 * c + q] + term
            return _

        lax.fori_loop(0, count, body, None, unroll=2)

    scale1, diag1, alpha1, beta1 = factors(1)

    def span(extent):
        return slice(WIDE - extent, WIDE + b1x + extent)

    def begin1(source, extent):
        f = source[span(extent + 1)]
        return alpha1 * ((2.0 - OMEGA) * f[1:-1] + beta1 * inner_sum(f))

    def sweep1(old, source, extent):
        v = old[span(extent + 1)]
        return (1.0 - OMEGA) * v[1:-1] + alpha1 * source[span(extent)] + beta1 * inner_sum(v)

    def residual1(source):
        v = v1[span(1)]
        r = source[span(0)] - diag1 * v[1:-1] + scale1 * inner_sum(v)
        r = r.reshape((b2x, 2) + r.shape[1:]).sum(1)
        sum1[...] = r
        r = (sum1[:, pl.ds(WIDE, b2y, stride=2), :] + sum1[:, pl.ds(WIDE + 1, b2y, stride=2), :]) * 0.125
        return r

    def coarse(k):
        level = k + 2
        scale, diagonal, alpha, beta = factors(level)
        f = fs[k][...]
        v = alpha * ((2.0 - OMEGA) * f + beta * wrap_sum(f))
        if k == n_levels - 1:
            vs[k][...] = v
            return
        r = f - diagonal * v + scale * wrap_sum(v)
        vs[k][...] = v
        rows = r.shape[1]
        us[k][...] = r.reshape((r.shape[0] // 2, 2) + r.shape[1:]).sum(1)
        r = us[k][:, pl.ds(0, rows // 2, stride=2), :] + us[k][:, pl.ds(1, rows // 2, stride=2), :]
        if rows == 8:
            r = jnp.concatenate([r, r], 1)
        fs[k + 1][...] = 0.125 * dot_lanes(r, mats[level - 1, 0])
        coarse(k + 1)
        c = dot_lanes(vs[k + 1][...], mats[level - 1, 1])[:, : rows // 2]
        ts[k][:, pl.ds(0, rows // 2, stride=2), :] = c
        ts[k][:, pl.ds(1, rows // 2, stride=2), :] = c
        c = ts[k][...]
        c = jnp.broadcast_to(c[:, None], (c.shape[0], 2) + c.shape[1:]).reshape(v.shape)
        v = vs[k][...] + c
        for sweep in range(2):
            v = (1.0 - OMEGA) * v + alpha * fs[k][...] + beta * wrap_sum(v)
        vs[k][...] = v

    lane = lax.broadcasted_iota(jnp.int32, (8, LANES), 1)
    me = ix * n_yb + iyb
    for wait in near:
        wait.wait()
    deal(HALO, bx, 4)
    begin0(va, HALO + 1, bx - 2)
    for wait in far:
        wait.wait()
    deal(HALO - SENT, SENT, SENT)
    deal(HALO + bx, SENT, SENT)
    begin0(va, HALO - SENT + 1, SENT)
    begin0(va, HALO + bx - 1, SENT)
    done = []
    for cycle in range(CYCLES):
        last = cycle == CYCLES - 1
        ahead = 4 if cycle == 0 else 0
        reach = 4 if last else 6
        rhs = residual0(va, ahead)
        low = WIDE - ahead // 2
        row1 = WIDE - ROWS // 2
        f1_here = f1.at[cycle]
        f1_here[pl.ds(WIDE, b1x), pl.ds(WIDE, b1y), :] = rhs[ahead // 2: ahead // 2 + b1x, WIDE - row1: WIDE - row1 + b1y]
        exchange = []
        for k, (dx, dy) in enumerate([(a, b) for a in (-1, 0, 1) for b in (-1, 0, 1) if (a, b) != (0, 0)]):
            planes = b1x if dx == 0 else reach
            from_x = WIDE + (b1x - reach if dx == 1 else 0)
            to_x = {-1: WIDE + b1x, 0: WIDE, 1: WIDE - reach}[dx]
            exchange.append(pltpu.make_async_remote_copy(
                src_ref=f1_here.at[pl.ds(from_x, planes), pl.ds(WIDE, b1y), :],
                dst_ref=f1_here.at[pl.ds(to_x, planes), pl.ds(WIDE - dy * b1y, b1y), :],
                send_sem=send1.at[cycle, k], recv_sem=recv1.at[cycle, k],
                device_id=place(ix + dx, iyb + dy), device_id_type=MESH))
        if cycle == 0:
            f1_local[pl.ds(low, rhs.shape[0]), pl.ds(row1, r0 // 2), :] = rhs
            down = f1_local
        else:
            for copy in exchange:
                copy.start()
            for copy in exchange:
                copy.wait_recv()
            down = f1_here
        v1[span(1)] = begin1(down, 1)
        rhs2 = dot_lanes(residual1(down).reshape(b2x * b2y, LANES), mats[0, 0])
        count = b2x * b2y // 2
        slots[cycle, me] = jnp.where(lane < LANES // 2, rhs2[:count], rhs2[count:])
        gather = []
        for k, (dx, dyb) in enumerate(peers):
            gather.append(pltpu.make_async_remote_copy(
                src_ref=slots.at[cycle, me], dst_ref=slots.at[cycle, me],
                send_sem=send2.at[cycle, k], recv_sem=recv2.at[cycle, me],
                device_id=place(ix + dx, iyb + dyb), device_id_type=MESH))
        for copy in gather:
            copy.start()
        if cycle == 0:
            for copy in exchange:
                copy.start()
        for dx, dyb in peers:
            who = lax.rem(ix + dx, n_gx) * n_yb + lax.rem(iyb + dyb, n_yb)
            slot = slots.at[cycle, who]
            pltpu.make_async_copy(slot, slot, recv2.at[cycle, who]).wait()
        for x in range(n_gx):
            for yb in range(n_yb):
                tile = slots[cycle, x * n_yb + yb]
                turned = roll(tile, LANES // 2, 1)
                parts = (jnp.where(lane < LANES // 2, tile, turned), jnp.where(lane < LANES // 2, turned, tile))
                for a in range(b2x):
                    part = parts[a // (b2x // 2)]
                    row = (a % (b2x // 2)) * b2y
                    fs[0][x * b2x + a, pl.ds(yb * b2y, b2y), :] = part[row: row + b2y]
        coarse(0)
        solved = dot_lanes(vs[0][...], mats[0, 1])
        for yb in range(n_yb):
            chunks[yb, :, pl.ds(0, b2y), :] = solved[:, yb * b2y:(yb + 1) * b2y]
        for a in range(2 * (WIDE // 2) + b2x):
            xa = lax.rem(ix * b2x - WIDE // 2 + a + nx2, nx2)
            for j in range(3):
                part = chunks[lax.rem(iyb + j - 1 + n_yb, n_yb), xa, pl.ds(0, b2y), :]
                window[a, pl.ds(j * b1y, b2y, stride=2), :] = part
                window[a, pl.ds(j * b1y + 1, b2y, stride=2), :] = part
        if cycle == 0:
            for copy in exchange:
                copy.wait_recv()
        top = reach - 1
        v = begin1(f1_here, top)
        first_plane, planes = WIDE - top, b1x + 2 * top
        wide = window[first_plane // 2: (first_plane + planes + 1) // 2]
        wide = jnp.broadcast_to(wide[:, None], (wide.shape[0], 2) + wide.shape[1:]).reshape((-1,) + wide.shape[1:])
        v1[span(top)] = v + wide[first_plane % 2: first_plane % 2 + planes]
        w1[span(top - 1)] = sweep1(v1, f1_here, top - 1)
        v1[span(top - 2)] = sweep1(w1, f1_here, top - 2)
        done += exchange + gather
        if last:
            correct0(va, 2)
            sweep0(va, vb, 1)
            sweep0(vb, va, 0)
        else:
            correct0(va, SENT - 1)
            sweep0(va, vb, SENT - 2)
            sweep0(vb, va, SENT - 3)
            sweep0(va, vb, SENT - 4)
            sweep0(vb, va, SENT - 5)

    def join(c, _):
        p = HALO + 4 * c
        value = jnp.concatenate([va[z, pl.ds(p, 4), pl.ds(ROWS, by), :] for z in range(2)], -1)
        value = dot_lanes(value, join_mat[...])
        staged[0, pl.ds(4 * c, 4)] = value[..., :half]
        staged[1, pl.ds(4 * c, 4)] = value[..., half:]
        return _

    lax.fori_loop(0, bx // 4, join, None, unroll=True)
    mine = pl.ds(pl.multiple_of(by * iz, 8), by)
    sent = pltpu.make_async_remote_copy(
        src_ref=staged.at[other], dst_ref=out_ref.at[:, mine, :], send_sem=send3.at[0], recv_sem=recv3.at[0],
        device_id=place(ix, iy * n_gz + other), device_id_type=MESH)
    sent.start()
    kept = pltpu.make_async_copy(staged.at[iz], out_ref.at[:, mine, :], recv3.at[1])
    kept.start()
    for copy in first + done:
        copy.wait_send()
    kept.wait()
    sent.wait()


def local(sizes, charge):
    n_gx, n_gy, n_gz = sizes
    bx, cy, cz = charge.shape
    by = cy // n_gz
    n_yb = n_gy * n_gz
    assert n_gz == 2 and cz == LANES and by % 16 == 0 and by // 4 * (bx // 4) == 16
    f32 = jnp.float32
    x0, r0 = bx + 2 * HALO, by + 2 * ROWS
    x1, r1 = bx // 2 + 2 * WIDE, by // 2 + 2 * WIDE
    nx2, ny2 = bx // 4 * n_gx, by // 4 * n_yb
    n_dev = n_gx * n_yb
    n_levels = LEVELS - 2
    shapes = [(nx2 >> k, max(8, ny2 >> k), LANES) for k in range(n_levels)]
    vmem = lambda *shape: pltpu.VMEM(shape, f32)
    level0 = vmem(2, x0, r0, LANES)
    nz = n_gz * cz
    scratch = [
        level0, level0, level0, level0,
        vmem(x0 // 2, r0, LANES), vmem(x0 // 2, r0, LANES),
        vmem(x1, r1, LANES), vmem(CYCLES, x1, r1, LANES), vmem(x1, r1, LANES), vmem(x1, r1, LANES),
        vmem(bx // 4, r1, LANES),
        vmem(CYCLES, n_dev, 8, LANES),
        vmem(n_yb, nx2, 8, LANES),
        vmem(bx // 4 + WIDE, r1, LANES),
        pltpu.VMEM((LEVELS - 2, 2, LANES, LANES), jnp.bfloat16),
        pltpu.VMEM((nz, nz), jnp.bfloat16), pltpu.VMEM((nz, nz), jnp.bfloat16),
        vmem(2, bx, by, LANES),
    ]
    scratch += [vmem(*s) for s in shapes] * 2
    halves = [vmem(max(1, s[0] // 2), s[1], s[2]) for s in shapes]
    scratch += halves * 2
    dma = lambda *shape: pltpu.SemaphoreType.DMA(shape)
    scratch += [dma(3, 4), dma(3, 2, 2), dma(CYCLES, 8), dma(CYCLES, 8),
                dma(CYCLES, n_dev), dma(CYCLES, n_dev), dma(1), dma(2)]
    return pl.pallas_call(
        functools.partial(kernel, sizes),
        out_shape=jax.ShapeDtypeStruct(charge.shape, f32),
        in_specs=[pl.BlockSpec(memory_space=pl.ANY)],
        out_specs=pl.BlockSpec(memory_space=pl.ANY),
        scratch_shapes=scratch,
        compiler_params=pltpu.CompilerParams(collective_id=0, has_side_effects=True),
    )(charge)


def solution(mesh):
    sizes = (mesh.shape["gx"], mesh.shape["gy"], mesh.shape["gz"])
    return jax.shard_map(
        functools.partial(local, sizes),
        mesh=mesh,
        in_specs=(P(("groups", "gx"), "gy", "gz"),),
        out_specs=P(("groups", "gx"), "gy", "gz"),
        check_vma=False,
    )
```

```python
import functools

import jax
import jax.numpy as jnp
from jax import lax
from jax.experimental import pallas as pl
from jax.experimental.pallas import tpu as pltpu
from jax.sharding import PartitionSpec as P

CYCLES = 2
LEVELS = 7

OMEGA = 2.0 / 3.0
SCREEN = 0.001

HALO = 8
SENT = 7
ROWS = 8
WIDE = 8
LANES = 128
MESH = pl.DeviceIdType.MESH


def factors(level):
    scale = 0.25**level
    diagonal = 6.0 * scale + SCREEN
    return scale, diagonal, OMEGA / diagonal, OMEGA * scale / diagonal


def roll(value, shift, axis):
    size = value.shape[axis]
    return value if size == 1 else pltpu.roll(value, shift % size, axis)


def split_dot(value, matrix):
    high = value.astype(jnp.bfloat16)
    low = (value - high.astype(jnp.float32)).astype(jnp.bfloat16)
    dot = functools.partial(jnp.dot, preferred_element_type=jnp.float32)
    return dot(high, matrix) + dot(low, matrix)


def dot_lanes(value, matrix):
    shape = value.shape
    out = split_dot(value.reshape(-1, shape[-1]), matrix)
    return out.reshape(shape[:-1] + (matrix.shape[-1],))


def indicator(rows, columns, rule):
    i = lax.broadcasted_iota(jnp.int32, (rows, columns), 0)
    j = lax.broadcasted_iota(jnp.int32, (rows, columns), 1)
    return jnp.where(rule(i, j), 1.0, 0.0).astype(jnp.bfloat16)


def plane_sum(value):
    last = value.ndim - 1
    total = roll(value, 1, last - 1) + roll(value, -1, last - 1)
    return total + (roll(value, 1, last) + roll(value, -1, last))


def inner_sum(value):
    return value[:-2] + value[2:] + plane_sum(value[1:-1])


def wrap_sum(value):
    if value.shape[0] == 1:
        beside = value + value
    else:
        beside = jnp.concatenate([value[-1:], value[:-1]], 0) + jnp.concatenate([value[1:], value[:1]], 0)
    return beside + plane_sum(value)


def kernel(sizes, charge_ref, out_ref, raw, src, va, vb, pairs, tall, f1_local, f1, v1, w1, sum1, slots,
           chunks, window, mats, split_mat, join_mat, staged, beside_x, *rest):
    n_gx, n_gy, n_gz = sizes
    n_levels = LEVELS - 2
    fs, vs, ts, us = (rest[k * n_levels:(k + 1) * n_levels] for k in range(4))
    (send0, recv0, send1, recv1, send2, recv2, send3, recv3, send4, recv4) = rest[4 * n_levels:]
    ix, iy, iz = lax.axis_index("gx"), lax.axis_index("gy"), lax.axis_index("gz")
    bx, cy, cz = charge_ref.shape
    by = cy // n_gz
    n_yb = n_gy * n_gz
    x0, r0 = bx + 2 * HALO, by + 2 * ROWS
    b1x, b1y = bx // 2, by // 2
    b2x, b2y = b1x // 2, b1y // 2
    nx2 = b2x * n_gx
    iyb = iy * n_gz + iz
    other = 1 - iz

    def place(x, yb):
        x = lax.rem(x + n_gx, n_gx)
        yb = lax.rem(yb + n_yb, n_yb)
        return {"gx": x, "gy": lax.div(yb, n_gz), "gz": lax.rem(yb, n_gz)}

    peers = [(dx, dyb) for dx in range(n_gx) for dyb in range(n_yb) if (dx, dyb) != (0, 0)]
    barrier = pltpu.get_barrier_semaphore()
    for dx, dyb in peers:
        pl.semaphore_signal(barrier, inc=1, device_id=place(ix + dx, iyb + dyb), device_id_type=MESH)
    pl.semaphore_wait(barrier, len(peers))

    hops = []
    first = [[], [], []]
    local_copies = [None, None, None]
    waits = [[], [], []]
    for k, dx in ((1, 0), (0, -1), (2, 1)):
        planes = bx if dx == 0 else SENT
        from_x = 0 if dx < 1 else bx - SENT
        to_x = {-1: HALO + bx, 0: HALO, 1: HALO - SENT}[dx]
        origin = charge_ref
        if dx != 0:
            origin = beside_x.at[k // 2]
            hops.append(pltpu.make_async_remote_copy(
                src_ref=charge_ref.at[pl.ds(from_x, planes), :, :], dst_ref=origin,
                send_sem=send4.at[k // 2], recv_sem=recv4.at[k // 2],
                device_id=place(ix + dx, iyb), device_id_type=MESH))
        for t, zt in enumerate((other, iz)):
            from_y = pl.multiple_of((by - ROWS) * zt, 8)
            to_y = pl.multiple_of(ROWS * (1 - zt), 8)
            source = origin.at[:, pl.ds(from_y, by + ROWS), :]
            target = raw.at[iz, pl.ds(to_x, planes), pl.ds(to_y, by + ROWS), :]
            if t == 1:
                local_copies[k] = pltpu.make_async_copy(source, target, recv0.at[k, 0, iz])
            else:
                first[k].append(pltpu.make_async_remote_copy(
                    src_ref=source, dst_ref=target, send_sem=send0.at[k, t], recv_sem=recv0.at[k, 0, iz],
                    device_id=place(ix, iy * n_gz + zt), device_id_type=MESH))
        for t, (step, from_y, to_y) in enumerate(((-1, 0, r0 - ROWS), (n_gz, cy - ROWS, 0))):
            first[k].append(pltpu.make_async_remote_copy(
                src_ref=origin.at[:, pl.ds(from_y, ROWS), :],
                dst_ref=raw.at[iz, pl.ds(to_x, planes), pl.ds(to_y, ROWS), :],
                send_sem=send0.at[k, 2 + t], recv_sem=recv0.at[k, 1, iz],
                device_id=place(ix, iy * n_gz + step), device_id_type=MESH))
        for z in range(n_gz):
            own = raw.at[z, pl.ds(to_x, planes), pl.ds(pl.multiple_of(ROWS * other, 8), by + ROWS), :]
            side = raw.at[z, pl.ds(to_x, planes), pl.ds(pl.multiple_of((r0 - ROWS) * iz, 8), ROWS), :]
            waits[k].append(pltpu.make_async_copy(own, own, recv0.at[k, 0, z]))
            waits[k].append(pltpu.make_async_copy(side, side, recv0.at[k, 1, z]))
    for copy in hops + first[1] + local_copies[1:2]:
        copy.start()
    near = waits[1]
    far = waits[0] + waits[2]

    nz = n_gz * cz
    half = nz // 2
    split_mat[...] = indicator(nz, nz, lambda i, j: i == jnp.where(j < half, 2 * j, 2 * (j - half) + 1))
    join_mat[...] = indicator(nz, nz, lambda i, j: j == jnp.where(i < half, 2 * i, 2 * (i - half) + 1))
    for level in range(1, LEVELS - 1):
        period = nz >> level
        mats[level - 1, 0] = indicator(
            LANES, LANES, lambda i, j: lax.div(i, 2) == (j & (period // 2 - 1)) + jnp.where(i < period, 0, LANES))
        mats[level - 1, 1] = indicator(LANES, LANES, lambda i, j: i == lax.div(j & (period - 1), 2))

    def deal(start, count, step):
        def body(c, _):
            planes = pl.ds(start + step * c, step)
            value = jnp.concatenate([raw[0, planes], raw[1, planes]], -1)
            value = dot_lanes(value, split_mat[...])
            src[0, planes] = value[..., :half]
            src[1, planes] = value[..., half:]
            return _

        lax.fori_loop(0, count // step, body, None, unroll=True)

    def neighbours(ref, p):
        even, odd = ref[0, p], ref[1, p]
        rows = lambda value: roll(value, 1, 0) + roll(value, -1, 0)
        sum_even = (ref[0, p - 1] + ref[0, p + 1]) + rows(even) + (odd + roll(odd, 1, 1))
        sum_odd = (ref[1, p - 1] + ref[1, p + 1]) + rows(odd) + (even + roll(even, -1, 1))
        return (even, odd), (sum_even, sum_odd)

    def over(extent, body):
        low = HALO - extent

        def pair(c, _):
            p = low + 2 * c
            body(p, c)
            return _

        lax.fori_loop(0, (bx + 2 * extent) // 2, pair, None, unroll=True)

    scale0, diag0, alpha0, beta0 = factors(0)

    def begin0(ref, start, count):
        def body(c, _):
            centre, beside = neighbours(src, start + c)
            for z in range(2):
                ref[z, start + c] = alpha0 * ((2.0 - OMEGA) * centre[z] + beta0 * beside[z])
            return _

        lax.fori_loop(0, count, body, None, unroll=7)

    def sweep0(old, new, extent):
        def body(p, c):
            for q in (p, p + 1):
                centre, beside = neighbours(old, q)
                for z in range(2):
                    new[z, q] = (1.0 - OMEGA) * centre[z] + alpha0 * src[z, q] + beta0 * beside[z]

        over(extent, body)

    def residual0(ref, extent):
        def body(p, c):
            total = None
            for q in (p, p + 1):
                centre, beside = neighbours(ref, q)
                for z in range(2):
                    term = src[z, q] - diag0 * centre[z] + scale0 * beside[z]
                    total = term if total is None else total + term
            pairs[c] = total

        over(extent, body)
        count = (bx + 2 * extent) // 2
        return 0.125 * (pairs[pl.ds(0, count), pl.ds(0, r0 // 2, stride=2), :]
                        + pairs[pl.ds(0, count), pl.ds(1, r0 // 2, stride=2), :])

    def correct0(ref, extent):
        low1 = WIDE - extent // 2 - extent % 2
        count = b1x + 2 * (WIDE - low1)
        row1 = WIDE - ROWS // 2
        value = v1[pl.ds(low1, count), pl.ds(row1, r0 // 2), :]
        tall[pl.ds(0, count), pl.ds(0, r0 // 2, stride=2), :] = value
        tall[pl.ds(0, count), pl.ds(1, r0 // 2, stride=2), :] = value
        start = HALO - 2 * (WIDE - low1)

        def body(c, _):
            term = tall[c]
            for q in range(2):
                for z in range(2):
                    ref[z, start + 2 * c + q] = ref[z, start + 2 * c + q] + term
            return _

        lax.fori_loop(0, count, body, None, unroll=2)

    scale1, diag1, alpha1, beta1 = factors(1)

    def span(extent):
        return slice(WIDE - extent, WIDE + b1x + extent)

    def begin1(source, extent):
        f = source[span(extent + 1)]
        return alpha1 * ((2.0 - OMEGA) * f[1:-1] + beta1 * inner_sum(f))

    def sweep1(old, source, extent):
        v = old[span(extent + 1)]
        return (1.0 - OMEGA) * v[1:-1] + alpha1 * source[span(extent)] + beta1 * inner_sum(v)

    def residual1(source):
        v = v1[span(1)]
        r = source[span(0)] - diag1 * v[1:-1] + scale1 * inner_sum(v)
        r = r.reshape((b2x, 2) + r.shape[1:]).sum(1)
        sum1[...] = r
        r = (sum1[:, pl.ds(WIDE, b2y, stride=2), :] + sum1[:, pl.ds(WIDE + 1, b2y, stride=2), :]) * 0.125
        return r

    def coarse(k):
        level = k + 2
        scale, diagonal, alpha, beta = factors(level)
        f = fs[k][...]
        v = alpha * ((2.0 - OMEGA) * f + beta * wrap_sum(f))
        if k == n_levels - 1:
            vs[k][...] = v
            return
        r = f - diagonal * v + scale * wrap_sum(v)
        vs[k][...] = v
        rows = r.shape[1]
        us[k][...] = r.reshape((r.shape[0] // 2, 2) + r.shape[1:]).sum(1)
        r = us[k][:, pl.ds(0, rows // 2, stride=2), :] + us[k][:, pl.ds(1, rows // 2, stride=2), :]
        if rows == 8:
            r = jnp.concatenate([r, r], 1)
        fs[k + 1][...] = 0.125 * dot_lanes(r, mats[level - 1, 0])
        coarse(k + 1)
        c = dot_lanes(vs[k + 1][...], mats[level - 1, 1])[:, : rows // 2]
        ts[k][:, pl.ds(0, rows // 2, stride=2), :] = c
        ts[k][:, pl.ds(1, rows // 2, stride=2), :] = c
        c = ts[k][...]
        c = jnp.broadcast_to(c[:, None], (c.shape[0], 2) + c.shape[1:]).reshape(v.shape)
        v = vs[k][...] + c
        for sweep in range(2):
            v = (1.0 - OMEGA) * v + alpha * fs[k][...] + beta * wrap_sum(v)
        vs[k][...] = v

    lane = lax.broadcasted_iota(jnp.int32, (8, LANES), 1)
    me = ix * n_yb + iyb
    for hop, k in zip(hops, (0, 2)):
        hop.wait_recv()
        for copy in first[k] + local_copies[k:k + 1]:
            copy.start()
    for wait in near:
        wait.wait()
    deal(HALO, bx, 4)
    begin0(va, HALO + 1, bx - 2)
    for wait in far:
        wait.wait()
    deal(HALO - SENT, SENT, SENT)
    deal(HALO + bx, SENT, SENT)
    begin0(va, HALO - SENT + 1, SENT)
    begin0(va, HALO + bx - 1, SENT)
    done = []
    for cycle in range(CYCLES):
        last = cycle == CYCLES - 1
        ahead = 4 if cycle == 0 else 0
        reach = 4 if last else 6
        rhs = residual0(va, ahead)
        low = WIDE - ahead // 2
        row1 = WIDE - ROWS // 2
        f1_here = f1.at[cycle]
        f1_here[pl.ds(WIDE, b1x), pl.ds(WIDE, b1y), :] = rhs[ahead // 2: ahead // 2 + b1x, WIDE - row1: WIDE - row1 + b1y]
        exchange = []
        for k, (dx, dy) in enumerate([(a, b) for a in (-1, 0, 1) for b in (-1, 0, 1) if (a, b) != (0, 0)]):
            planes = b1x if dx == 0 else reach
            from_x = WIDE + (b1x - reach if dx == 1 else 0)
            to_x = {-1: WIDE + b1x, 0: WIDE, 1: WIDE - reach}[dx]
            exchange.append(pltpu.make_async_remote_copy(
                src_ref=f1_here.at[pl.ds(from_x, planes), pl.ds(WIDE, b1y), :],
                dst_ref=f1_here.at[pl.ds(to_x, planes), pl.ds(WIDE - dy * b1y, b1y), :],
                send_sem=send1.at[cycle, k], recv_sem=recv1.at[cycle, k],
                device_id=place(ix + dx, iyb + dy), device_id_type=MESH))
        if cycle == 0:
            f1_local[pl.ds(low, rhs.shape[0]), pl.ds(row1, r0 // 2), :] = rhs
            down = f1_local
        else:
            for copy in exchange:
                copy.start()
            for copy in exchange:
                copy.wait_recv()
            down = f1_here
        v1[span(1)] = begin1(down, 1)
        rhs2 = dot_lanes(residual1(down).reshape(b2x * b2y, LANES), mats[0, 0])
        count = b2x * b2y // 2
        slots[cycle, me] = jnp.where(lane < LANES // 2, rhs2[:count], rhs2[count:])
        gather = []
        for k, (dx, dyb) in enumerate(peers):
            gather.append(pltpu.make_async_remote_copy(
                src_ref=slots.at[cycle, me], dst_ref=slots.at[cycle, me],
                send_sem=send2.at[cycle, k], recv_sem=recv2.at[cycle, me],
                device_id=place(ix + dx, iyb + dyb), device_id_type=MESH))
        for copy in gather:
            copy.start()
        if cycle == 0:
            for copy in exchange:
                copy.start()
        for dx, dyb in peers:
            who = lax.rem(ix + dx, n_gx) * n_yb + lax.rem(iyb + dyb, n_yb)
            slot = slots.at[cycle, who]
            pltpu.make_async_copy(slot, slot, recv2.at[cycle, who]).wait()
        for x in range(n_gx):
            for yb in range(n_yb):
                tile = slots[cycle, x * n_yb + yb]
                turned = roll(tile, LANES // 2, 1)
                parts = (jnp.where(lane < LANES // 2, tile, turned), jnp.where(lane < LANES // 2, turned, tile))
                for a in range(b2x):
                    part = parts[a // (b2x // 2)]
                    row = (a % (b2x // 2)) * b2y
                    fs[0][x * b2x + a, pl.ds(yb * b2y, b2y), :] = part[row: row + b2y]
        coarse(0)
        solved = dot_lanes(vs[0][...], mats[0, 1])
        for yb in range(n_yb):
            chunks[yb, :, pl.ds(0, b2y), :] = solved[:, yb * b2y:(yb + 1) * b2y]
        for a in range(2 * (WIDE // 2) + b2x):
            xa = lax.rem(ix * b2x - WIDE // 2 + a + nx2, nx2)
            for j in range(3):
                part = chunks[lax.rem(iyb + j - 1 + n_yb, n_yb), xa, pl.ds(0, b2y), :]
                window[a, pl.ds(j * b1y, b2y, stride=2), :] = part
                window[a, pl.ds(j * b1y + 1, b2y, stride=2), :] = part
        if cycle == 0:
            for copy in exchange:
                copy.wait_recv()
        top = reach - 1
        v = begin1(f1_here, top)
        first_plane, planes = WIDE - top, b1x + 2 * top
        wide = window[first_plane // 2: (first_plane + planes + 1) // 2]
        wide = jnp.broadcast_to(wide[:, None], (wide.shape[0], 2) + wide.shape[1:]).reshape((-1,) + wide.shape[1:])
        v1[span(top)] = v + wide[first_plane % 2: first_plane % 2 + planes]
        w1[span(top - 1)] = sweep1(v1, f1_here, top - 1)
        v1[span(top - 2)] = sweep1(w1, f1_here, top - 2)
        done += exchange + gather
        if last:
            correct0(va, 2)
            sweep0(va, vb, 1)
            sweep0(vb, va, 0)
        else:
            correct0(va, SENT - 1)
            sweep0(va, vb, SENT - 2)
            sweep0(vb, va, SENT - 3)
            sweep0(va, vb, SENT - 4)
            sweep0(vb, va, SENT - 5)

    def join(c, _):
        p = HALO + 4 * c
        value = jnp.concatenate([va[z, pl.ds(p, 4), pl.ds(ROWS, by), :] for z in range(2)], -1)
        value = dot_lanes(value, join_mat[...])
        staged[0, pl.ds(4 * c, 4)] = value[..., :half]
        staged[1, pl.ds(4 * c, 4)] = value[..., half:]
        return _

    lax.fori_loop(0, bx // 4, join, None, unroll=True)
    mine = pl.ds(pl.multiple_of(by * iz, 8), by)
    sent = pltpu.make_async_remote_copy(
        src_ref=staged.at[other], dst_ref=out_ref.at[:, mine, :], send_sem=send3.at[0], recv_sem=recv3.at[0],
        device_id=place(ix, iy * n_gz + other), device_id_type=MESH)
    sent.start()
    kept = pltpu.make_async_copy(staged.at[iz], out_ref.at[:, mine, :], recv3.at[1])
    kept.start()
    for copy in hops + first[0] + first[1] + first[2] + done:
        copy.wait_send()
    kept.wait()
    sent.wait()


def local(sizes, charge):
    n_gx, n_gy, n_gz = sizes
    bx, cy, cz = charge.shape
    by = cy // n_gz
    n_yb = n_gy * n_gz
    assert n_gz == 2 and cz == LANES and by % 16 == 0 and by // 4 * (bx // 4) == 16
    f32 = jnp.float32
    x0, r0 = bx + 2 * HALO, by + 2 * ROWS
    x1, r1 = bx // 2 + 2 * WIDE, by // 2 + 2 * WIDE
    nx2, ny2 = bx // 4 * n_gx, by // 4 * n_yb
    n_dev = n_gx * n_yb
    n_levels = LEVELS - 2
    shapes = [(nx2 >> k, max(8, ny2 >> k), LANES) for k in range(n_levels)]
    vmem = lambda *shape: pltpu.VMEM(shape, f32)
    level0 = vmem(2, x0, r0, LANES)
    nz = n_gz * cz
    scratch = [
        level0, level0, level0, level0,
        vmem(x0 // 2, r0, LANES), vmem(x0 // 2, r0, LANES),
        vmem(x1, r1, LANES), vmem(CYCLES, x1, r1, LANES), vmem(x1, r1, LANES), vmem(x1, r1, LANES),
        vmem(bx // 4, r1, LANES),
        vmem(CYCLES, n_dev, 8, LANES),
        vmem(n_yb, nx2, 8, LANES),
        vmem(bx // 4 + WIDE, r1, LANES),
        pltpu.VMEM((LEVELS - 2, 2, LANES, LANES), jnp.bfloat16),
        pltpu.VMEM((nz, nz), jnp.bfloat16), pltpu.VMEM((nz, nz), jnp.bfloat16),
        vmem(2, bx, by, LANES),
        vmem(2, SENT, cy, LANES),
    ]
    scratch += [vmem(*s) for s in shapes] * 2
    halves = [vmem(max(1, s[0] // 2), s[1], s[2]) for s in shapes]
    scratch += halves * 2
    dma = lambda *shape: pltpu.SemaphoreType.DMA(shape)
    scratch += [dma(3, 4), dma(3, 2, 2), dma(CYCLES, 8), dma(CYCLES, 8),
                dma(CYCLES, n_dev), dma(CYCLES, n_dev), dma(1), dma(2), dma(2), dma(2)]
    return pl.pallas_call(
        functools.partial(kernel, sizes),
        out_shape=jax.ShapeDtypeStruct(charge.shape, f32),
        in_specs=[pl.BlockSpec(memory_space=pl.ANY)],
        out_specs=pl.BlockSpec(memory_space=pl.ANY),
        scratch_shapes=scratch,
        compiler_params=pltpu.CompilerParams(collective_id=0, has_side_effects=True),
    )(charge)


def solution(mesh):
    sizes = (mesh.shape["gx"], mesh.shape["gy"], mesh.shape["gz"])
    return jax.shard_map(
        functools.partial(local, sizes),
        mesh=mesh,
        in_specs=(P(("groups", "gx"), "gy", "gz"),),
        out_specs=P(("groups", "gx"), "gy", "gz"),
        check_vma=False,
    )
```
